32 devices in a mesh: lon: 8 (over z, y), lat: 4 (over x, core).
Axes of the slice: x: 2, y: 2, z: 4, core: 2. Of those that a mesh axis runs over, the one named last changes fastest.
Arguments:
- right_side: float32 [1024, 4096], P('lat', 'lon'), may hold values from -6 to 6
- depth_level: int32 [1024, 4096], P('lat', 'lon'), may hold values from 1 to 50
- ocean_mask: int32 [1024, 4096], P('lat', 'lon'), may hold values 0 or 1
Outputs:
- pressure: float32 [1024, 4096], P('lat', 'lon')
- residual: float32 [1024, 4096], P('lat', 'lon')
The draws below stay inside these ranges and needn't reach their ends.
All inputs are finite; a program needn't handle non-finite values. No bound on the sum of `ocean_mask` on one device may be relied on, other than what follows from the above.
Results may differ from the reference program's by a relative error of at most 0.0003.
Values sent between devices are 32-bit elements; how exact they have to be, the bound alone decides.
A program may use at most 128 MiB of HBM per device.

```python
import jax
import jax.numpy as jnp

LEVELS = 4
SWEEPS = 2
COARSE_SWEEPS = 9
DEPTH_LEVELS = 50
NLAT = 1024
NLON = 4096


def place_ends(result, key, least, high):
    place = [jax.random.randint(jax.random.fold_in(key, axis), (), 0, length) for axis, length in enumerate(result.shape)]
    main_axis = result.shape.index(max(result.shape))
    next_to = place[:main_axis] + [(place[main_axis] + 1) % result.shape[main_axis]] + place[main_axis + 1:]
    return result.at[tuple(place)].set(least).at[tuple(next_to)].set(high)


def level_of(rng, shape, pieces, least, high):
    def one(dim, blocks):
        draws = jax.random.uniform(jax.random.fold_in(jax.random.fold_in(rng, 6), dim), (blocks,), jnp.float32, least / len(pieces), high / len(pieces))
        return jnp.repeat(jnp.exp(draws), shape[dim] // blocks).reshape((-1,) + (1,) * (len(shape) - dim - 1))

    gain = one(*pieces[0])
    for cut in pieces[1:]:
        gain = gain * one(*cut)
    return gain


def bell_draw(key, dims, deviation, most, pieces=(), kind=jnp.bfloat16):
    entries = deviation * jax.random.normal(key, dims, jnp.float32)
    if pieces:
        entries = entries * level_of(key, dims, pieces, -0.22, 0.18)
    return jnp.clip(entries, -most, most).astype(kind)


def setup_inputs(seed: int = 0) -> dict:
    splits = jax.random.split(jax.random.key(seed), 4)
    return {
        "right_side": bell_draw(splits[0], (NLAT, NLON), 1.0, 6.0, ((0, 4), (1, 8)), jnp.float32),
        "depth_level": place_ends(jax.random.randint(splits[1], (NLAT, NLON), 1, DEPTH_LEVELS + 1), jax.random.fold_in(splits[1], 1), 1, DEPTH_LEVELS).astype(jnp.int32),
        "ocean_mask": place_ends((jax.random.randint(splits[2], (NLAT, NLON), 0, 4) < 3).astype(jnp.int32), jax.random.fold_in(splits[2], 1), 0, 1),
    }


OMEGA = 0.8
SIGMA = 1e-5


def neighbours(field):
    east_side = jnp.roll(field, -1, axis=1)
    west_side = jnp.roll(field, 1, axis=1)
    zero_row = jnp.zeros((1, field.shape[1]), field.dtype)
    north_side = jnp.concatenate([field[1:], zero_row], axis=0)
    south_side = jnp.concatenate([zero_row, field[:-1]], axis=0)
    return east_side, west_side, north_side, south_side


def coefficients(height, scale):
    east_side, west_side, north_side, south_side = neighbours(height)
    coef_east = jnp.minimum(height, east_side) * scale
    coef_west = jnp.minimum(height, west_side) * scale
    coef_north = jnp.minimum(height, north_side) * scale
    coef_south = jnp.minimum(height, south_side) * scale
    faces = coef_east + coef_west + coef_north + coef_south
    diagonal = SIGMA + faces
    return coef_east, coef_west, coef_north, coef_south, diagonal, faces


def keep_active(source, coefs):
    return jnp.where(coefs[5] > 0.0, source, jnp.zeros_like(source))


def operate(field, coefs):
    east_side, west_side, north_side, south_side = neighbours(field)
    return coefs[4] * field - coefs[0] * east_side - coefs[1] * west_side - coefs[2] * north_side - coefs[3] * south_side


def jacobi(field, source, coefs):
    return field + OMEGA * (source - operate(field, coefs)) / coefs[4]


def smooth_zero(source, coefs, count):
    field = OMEGA * source / coefs[4]
    for sweep in range(count - 1):
        field = jacobi(field, source, coefs)
    return field


def restrict(field):
    row_count, col_count = field.shape
    return field.reshape(row_count // 2, 2, col_count // 2, 2).mean(axis=(1, 3))


def prolong(field):
    row_count, col_count = field.shape
    return jnp.broadcast_to(field[:, None, :, None], (row_count, 2, col_count, 2)).reshape(row_count * 2, col_count * 2)


def reference(right_side, depth_level, ocean_mask):
    ocean = ocean_mask.astype(jnp.float32)
    height = ocean * depth_level.astype(jnp.float32) / DEPTH_LEVELS
    source = right_side
    saved = []
    for level in range(LEVELS - 1):
        coefs = coefficients(height, 0.25 ** level)
        source = keep_active(source, coefs)
        iterate = smooth_zero(source, coefs, SWEEPS)
        saved.append((iterate, source, coefs))
        source = restrict(source - operate(iterate, coefs))
        height = restrict(height)
    coefs = coefficients(height, 0.25 ** (LEVELS - 1))
    source = keep_active(source, coefs)
    iterate = smooth_zero(source, coefs, COARSE_SWEEPS)
    for level in reversed(range(LEVELS - 1)):
        previous, source, coefs = saved[level]
        iterate = previous + prolong(iterate)
        for sweep in range(SWEEPS):
            iterate = jacobi(iterate, source, coefs)
    source, coefs = saved[0][1], saved[0][2]
    return iterate, source - operate(iterate, coefs)
```

```python
import functools

import jax
import jax.numpy as jnp
from jax import lax
from jax.experimental import pallas as pl
from jax.experimental.pallas import tpu as pltpu
from jax.sharding import PartitionSpec as P

DEPTH_LEVELS = 50
COARSE_SWEEPS = 9
OMEGA = 0.8
SIGMA = 1e-05
HALO = 16
DEEP = 24
DEEP_LANES = 32
MESH = pl.DeviceIdType.MESH
F32 = jnp.float32
BF16 = jnp.bfloat16


def lanes_of(shape=(8, 128)):
    return lax.broadcasted_iota(jnp.int32, shape, 1)


def east_of(tiles):
    if len(tiles) == 1:
        return [pltpu.roll(tiles[0], 127, 1)]
    lane = lanes_of()
    turned = [pltpu.roll(x, 127, 1) for x in tiles]
    return [jnp.where(lane == 127, turned[(t + 1) % len(tiles)], turned[t]) for t in range(len(tiles))]


def west_of(tiles):
    if len(tiles) == 1:
        return [pltpu.roll(tiles[0], 1, 1)]
    lane = lanes_of()
    turned = [pltpu.roll(x, 1, 1) for x in tiles]
    return [jnp.where(lane == 0, turned[t - 1], turned[t]) for t in range(len(tiles))]


def upper(x):
    return pltpu.roll(x, 7, 0)


def lower(x):
    return pltpu.roll(x, 1, 0)


def at(j):
    start = (j + 1) * 8
    return pl.ds(start if isinstance(start, int) else pl.multiple_of(start, 8), 8)


def load(ref, j):
    return [ref[t, at(j), :] for t in range(ref.shape[0])]


def store(ref, j, tiles):
    for t, x in enumerate(tiles):
        ref[t, at(j), :] = x


def each(count, unroll, body):
    if unroll >= count:
        for j in range(count):
            body(j)
    else:
        lax.fori_loop(0, count, lambda j, c: (body(j), c)[1], 0, unroll=unroll)


def wrap(ref, count):
    store(ref, -1, [lower(x) for x in load(ref, count - 1)])
    store(ref, count, [upper(x) for x in load(ref, 0)])


def split_dot(x, mat, parts):
    total = None
    for part in range(parts):
        piece = x.astype(BF16)
        term = jnp.dot(piece, mat, preferred_element_type=F32)
        total = term if total is None else total + term
        if part < parts - 1:
            x = x - piece.astype(F32)
    return total


def shrink(tiles, mats, parts):
    outs = []
    for p in range(len(tiles) // 2):
        outs.append(split_dot(tiles[2 * p], mats[0], parts) + split_dot(tiles[2 * p + 1], mats[1], parts))
    if len(tiles) % 2:
        outs.append(split_dot(tiles[-1], mats[2], parts))
    return outs


def spread(tiles, mats, fine_count, parts):
    outs = []
    for p in range(fine_count // 2):
        outs += [split_dot(tiles[p], mats[3], parts), split_dot(tiles[p], mats[4], parts)]
    if fine_count % 2:
        outs.append(split_dot(tiles[fine_count // 2], mats[5], parts))
    return outs


class Level:
    def __init__(self, index, count, unroll, refs):
        self.scale = 0.0625**index / DEPTH_LEVELS
        self.count, self.unroll = count, unroll
        self.h, self.s, self.ke, self.kn, self.w, self.d, self.a, self.b, self.half = refs

    def coefficients(self):
        wrap(self.h, self.count)

        def body(j):
            h = load(self.h, j)
            ke = [jnp.minimum(x, y) * self.scale for x, y in zip(h, east_of(h))]
            kw = west_of(ke)
            kn = [jnp.minimum(x, y) * self.scale for x, y in zip(h, load(self.h, j + 1))]
            ks = [jnp.minimum(x, y) * self.scale for x, y in zip(h, load(self.h, j - 1))]
            faces = [a + b + c + d for a, b, c, d in zip(ke, kw, kn, ks)]
            diag = [SIGMA + f for f in faces]
            w = [OMEGA / d for d in diag]
            s = [jnp.where(f > 0.0, x, 0.0) for f, x in zip(faces, load(self.s, j))]
            for ref, value in ((self.ke, ke), (self.kn, kn), (self.w, w), (self.d, diag), (self.s, s)):
                store(ref, j, value)
            store(self.a, j, [x * y for x, y in zip(w, s)])

        each(self.count, self.unroll, body)
        wrap(self.kn, self.count)

    def pulled(self, ref, j):
        v, ke = load(ref, j), load(self.ke, j)
        flow = west_of([x * y for x, y in zip(ke, v)])
        rows = zip(ke, east_of(v), flow, load(self.kn, j), load(ref, j + 1), load(self.kn, j - 1), load(ref, j - 1))
        return v, [k * e + f + n * vn + s * vs for k, e, f, n, vn, s, vs in rows]

    def sweep(self, src, dst):
        wrap(src, self.count)

        def body(j):
            v, acc = self.pulled(src, j)
            new = [(1.0 - OMEGA) * x + w * (s + a) for x, w, s, a in zip(v, load(self.w, j), load(self.s, j), acc)]
            store(dst, j, new)

        each(self.count, self.unroll, body)

    def residual(self, ref, j):
        v, acc = self.pulled(ref, j)
        return [s - d * x + a for s, d, x, a in zip(load(self.s, j), load(self.d, j), v, acc)]

    def halve(self, rows_of, factor):
        def body(j):
            for t, (x, y) in enumerate(zip(rows_of(2 * j), rows_of(2 * j + 1))):
                start = j * 8 if isinstance(j, int) else pl.multiple_of(j * 8, 8)
                self.half[t, pl.ds(start, 8), :] = (x + y) * factor

        each(self.count // 2, self.unroll // 2, body)

    def down(self):
        self.coefficients()
        self.sweep(self.a, self.b)
        wrap(self.b, self.count)
        self.halve(lambda j: self.residual(self.b, j), 0.25)

    def up(self):
        def body(j):
            start = j * 8 if isinstance(j, int) else pl.multiple_of(j * 8, 8)
            extra = [self.half[t, pl.ds(start, 8), :] for t in range(self.half.shape[0])]
            for i in (2 * j, 2 * j + 1):
                store(self.b, i, [x + y for x, y in zip(load(self.b, i), extra)])

        each(self.count // 2, self.unroll // 2, body)
        self.sweep(self.b, self.a)
        self.sweep(self.a, self.b)


class Exchange:
    def __init__(self, x, halo, width, refs, sems):
        self.x, self.halo, self.width = x, halo, width
        self.pack, self.got, self.corner = refs
        self.sems = sems
        self.tiles = x.shape[1] - 1
        self.n = x.shape[2] - 2 * halo
        self.groups = 128 // width

    def fill(self, f):
        lane = lanes_of()
        for side in range(2):
            for m in range(self.n // 8 // self.groups):
                total = None
                for g in range(self.groups):
                    row = self.halo + 8 * (m * self.groups + g)
                    chunk = self.x[f, 0 if side == 0 else self.tiles - 1, row : row + 8, :]
                    shift = (self.width * g + side * self.width) % 128
                    chunk = pltpu.roll(chunk, shift, 1) if shift else chunk
                    total = chunk if total is None else jnp.where(lane >= self.width * g, chunk, total)
                self.pack[side, f, 8 * m : 8 * m + 8, :] = total

    def start(self, place):
        lat, lon, nlat, nlon = place
        copies = []

        def send(src, dst, dlat, dlon):
            k = len(copies)
            copy = pltpu.make_async_remote_copy(
                src_ref=src,
                dst_ref=dst,
                send_sem=self.sems.at[0, k],
                recv_sem=self.sems.at[1, k],
                device_id={"lat": lax.rem(lat + dlat + nlat, nlat), "lon": lax.rem(lon + dlon + nlon, nlon)},
                device_id_type=MESH,
            )
            copy.start()
            copies.append(copy)

        h, n, last = self.halo, self.n, self.pack.shape[2] - 8
        for side, dlon in ((0, -1), (1, 1)):
            send(self.pack.at[side], self.got.at[side], 0, dlon)
        for side, dlon in ((0, -1), (1, 1)):
            send(self.pack.at[side, :, pl.ds(last, 8), :], self.corner.at[side], 1, dlon)
            send(self.pack.at[side, :, pl.ds(0, 8), :], self.corner.at[2 + side], -1, dlon)
        core = pl.ds(0, self.tiles)
        send(self.x.at[:, core, pl.ds(n, h), :], self.x.at[:, core, pl.ds(0, h), :], 1, 0)
        send(self.x.at[:, core, pl.ds(h, h), :], self.x.at[:, core, pl.ds(h + n, h), :], -1, 0)
        self.copies = copies

    def finish(self, place):
        lat, lon, nlat, nlon = place
        for copy in self.copies:
            copy.wait()
        lane = lanes_of()
        edge, total = self.halo // 8, self.x.shape[2] // 8
        count = self.n // 8
        for f in range(2):
            for b in range(total):
                a = b - edge
                if a < 0:
                    a, refs = a + count, (self.corner.at[0, f], self.corner.at[1, f])
                    start = 0
                elif a >= count:
                    a, refs = a - count, (self.corner.at[2, f], self.corner.at[3, f])
                    start = 0
                else:
                    start = 8 * (a // self.groups)
                    refs = (self.got.at[0, f], self.got.at[1, f])
                g = a % self.groups
                east, west = refs[0][start : start + 8, :], refs[1][start : start + 8, :]
                shift = (128 - self.width * g) % 128
                east = pltpu.roll(east, shift, 1) if shift else east
                shift = (256 - self.width - self.width * g) % 128
                west = pltpu.roll(west, shift, 1) if shift else west
                tile = jnp.where(lane < self.width, east, jnp.where(lane >= 128 - self.width, west, 0.0))
                self.x[f, self.tiles, 8 * b : 8 * b + 8, :] = tile
        for blocks, pole in ((range(edge), lat == 0), (range(total - edge, total), lat == nlat - 1)):
            keep = jnp.where(pole, 0.0, 1.0)
            for f in range(2):
                for t in range(self.tiles + 1):
                    for b in blocks:
                        self.x[f, t, 8 * b : 8 * b + 8, :] = self.x[f, t, 8 * b : 8 * b + 8, :] * keep


def kernel(place_of, right_hbm, depth_hbm, mask_hbm, press_hbm, resid_hbm, x0, depth, mask, mats, x2, y2, z2, c1, *rest):
    nlat, nlon = place_of
    pack0, got0, corner0, pack2, got2, corner2, sems0, sems2, in_sems, out_sems = rest[:10]
    refs0, refs1, refs2 = rest[10:19], rest[19:28], rest[28:37]
    lat, lon = lax.axis_index("lat"), lax.axis_index("lon")
    place = (lat, lon, nlat, nlon)
    rows = depth.shape[1]
    tiles = depth.shape[0]

    loads = []
    for t in range(tiles):
        cols = pl.ds(128 * t, 128)
        for i, (src, dst) in enumerate(
            (
                (depth_hbm.at[:, cols], depth.at[t]),
                (mask_hbm.at[:, cols], mask.at[t]),
                (right_hbm.at[:, cols], x0.at[1, t, pl.ds(HALO, rows), :]),
            )
        ):
            loads.append(pltpu.make_async_copy(src, dst, in_sems.at[i, t]))
            loads[-1].start()

    barrier = pltpu.get_barrier_semaphore()
    for dlat in (-1, 0, 1):
        for dlon in (-1, 0, 1):
            if dlat or dlon:
                pl.semaphore_signal(
                    barrier,
                    inc=1,
                    device_id={"lat": lax.rem(lat + dlat + nlat, nlat), "lon": lax.rem(lon + dlon + nlon, nlon)},
                    device_id_type=MESH,
                )

    fine = lax.broadcasted_iota(jnp.int32, (128, 128), 0)
    coarse = lanes_of((128, 128))
    for base, f, c in ((0, fine, coarse), (3, coarse, fine)):
        first = jnp.right_shift(f, 1)
        for i, target in enumerate((first, first + 64, jnp.where(f < 64, first, first + 64))):
            mats[base + i] = jnp.where(target == c, 1.0, 0.0).astype(BF16)
    mats = [mats[i] for i in range(6)]

    for copy in loads:
        copy.wait()
    for t in range(tiles):
        x0[0, t, HALO : HALO + rows, :] = (depth[t] * mask[t]).astype(F32)
    outer = Exchange(x0, HALO, HALO, (pack0, got0, corner0), sems0)
    outer.fill(0)
    outer.fill(1)
    pl.semaphore_wait(barrier, 8)
    outer.start(place)
    outer.finish(place)

    count0 = refs0[0].shape[1] // 8 - 2
    count1 = refs1[0].shape[1] // 8 - 2
    count2 = refs2[0].shape[1] // 8 - 2
    level0 = Level(0, count0, 4, refs0)
    level1 = Level(1, count1, 6, refs1)
    level2 = Level(2, count2, count2, refs2)
    for j in range(count0):
        for t in range(tiles + 1):
            level0.h[t, at(j), :] = x0[0, t, pl.ds(j, 8, stride=count0), :]
            level0.s[t, at(j), :] = x0[1, t, pl.ds(j, 8, stride=count0), :]

    level0.halve(lambda j: load(level0.h, j), 1.0)
    for t, x in enumerate(shrink([level0.half[t] for t in range(tiles + 1)], mats, 1)):
        level1.h[t, 8 : 8 + 8 * count1, :] = x
    level0.down()
    for t, x in enumerate(shrink([level0.half[t] for t in range(tiles + 1)], mats, 3)):
        level1.s[t, 8 : 8 + 8 * count1, :] = x

    half1 = count1 // 2
    margin = HALO // 4
    deep_rows = x2.shape[2] - 2 * DEEP

    def pass_down(f, parts):
        out = shrink([level1.half[0], level1.half[1]], mats, parts)[0]
        for j in range(half1):
            y2[pl.ds(j, 8, stride=half1), :] = out[8 * j : 8 * j + 8]
        for a in range(deep_rows // 8):
            x2[f, 0, DEEP + 8 * a : DEEP + 8 * a + 8, :] = y2[margin + 8 * a : margin + 8 * a + 8, :]

    level1.halve(lambda j: load(level1.h, j), 1.0)
    pass_down(0, 2)
    level1.down()
    pass_down(1, 3)

    inner = Exchange(x2, DEEP, DEEP_LANES, (pack2, got2, corner2), sems2)
    inner.fill(0)
    inner.fill(1)
    inner.start(place)
    inner.finish(place)
    for j in range(count2):
        for t in range(2):
            level2.h[t, at(j), :] = x2[0, t, pl.ds(j, 8, stride=count2), :]
            level2.s[t, at(j), :] = x2[1, t, pl.ds(j, 8, stride=count2), :]
    count3 = count2 // 2
    level2.halve(lambda j: load(level2.h, j), 1.0)
    height = shrink([level2.half[0], level2.half[1]], mats, 2)[0]
    level2.down()
    source = shrink([level2.half[0], level2.half[1]], mats, 3)[0]

    scale = 0.0625**3 / DEPTH_LEVELS
    h = [height[8 * j : 8 * j + 8] for j in range(count3)]
    s = [source[8 * j : 8 * j + 8] for j in range(count3)]

    def north(v):
        return v[1:] + [upper(v[0])]

    ke = [jnp.minimum(x, pltpu.roll(x, 127, 1)) * scale for x in h]
    kn = [jnp.minimum(x, y) * scale for x, y in zip(h, north(h))]
    ks = [lower(kn[-1])] + kn[:-1]
    faces = [a + pltpu.roll(a, 1, 1) + b + c for a, b, c in zip(ke, kn, ks)]
    w = [OMEGA / (SIGMA + f) for f in faces]
    s = [jnp.where(f > 0.0, x, 0.0) for f, x in zip(faces, s)]
    v = [x * y for x, y in zip(w, s)]
    for _ in range(COARSE_SWEEPS - 1):
        up, down = north(v), [lower(v[-1])] + v[:-1]
        v = [
            (1.0 - OMEGA) * v[j]
            + w[j]
            * (s[j] + ke[j] * pltpu.roll(v[j], 127, 1) + pltpu.roll(ke[j] * v[j], 1, 1) + kn[j] * up[j] + ks[j] * down[j])
            for j in range(count3)
        ]

    for t, x in enumerate(spread([jnp.concatenate(v, axis=0)], mats, 2, 3)):
        level2.half[t] = x
    level2.up()
    for j in range(count2):
        for t in range(2):
            z2[t, pl.ds(j, 8, stride=count2), :] = level2.b[t, at(j), :]
    for j in range(half1):
        for t in range(2):
            c1[t, 8 * j : 8 * j + 8, :] = z2[t, pl.ds(DEEP - margin + j, 8, stride=half1), :]
    for t, x in enumerate(spread([c1[0], c1[1]], mats, 3, 3)):
        level1.half[t] = x
    level1.up()
    body = pl.ds(8, 8 * count1)
    for t, x in enumerate(spread([level1.b[t, body, :] for t in range(3)], mats, tiles + 1, 3)):
        level0.half[t] = x
    level0.up()
    wrap(level0.b, count0)
    each(count0, 4, lambda j: store(level0.a, j, level0.residual(level0.b, j)))

    stores = []
    for i, (ref, out) in enumerate(((level0.b, press_hbm), (level0.a, resid_hbm))):
        for t in range(tiles):
            for j in range(count0):
                x0[i, t, pl.ds(j, 8, stride=count0), :] = ref[t, at(j), :]
            stores.append(
                pltpu.make_async_copy(
                    x0.at[i, t, pl.ds(HALO, rows), :], out.at[:, pl.ds(128 * t, 128)], out_sems.at[i, t]
                )
            )
            stores[-1].start()
    for copy in stores:
        copy.wait()


def solution(mesh):
    nlat, nlon = mesh.shape["lat"], mesh.shape["lon"]

    def local(right_side, depth_level, ocean_mask):
        rows, columns = right_side.shape
        tiles = columns // 128
        ext = rows + 2 * HALO
        deep = rows // 4 + 2 * DEEP

        def level_refs(tiles, total):
            full = pltpu.VMEM((tiles, total + 16, 128), F32)
            return [full] * 8 + [pltpu.VMEM((tiles, total // 2, 128), F32)]

        def exchange_refs(n, width):
            packed = pltpu.VMEM((2, 2, n * width // 128, 128), F32)
            return [packed, packed, pltpu.VMEM((4, 2, 8, 128), F32)]

        return pl.pallas_call(
            functools.partial(kernel, (nlat, nlon)),
            out_shape=[jax.ShapeDtypeStruct((rows, columns), F32)] * 2,
            in_specs=[pl.BlockSpec(memory_space=pl.ANY)] * 3,
            out_specs=[pl.BlockSpec(memory_space=pl.ANY)] * 2,
            scratch_shapes=[
                pltpu.VMEM((2, tiles + 1, ext, 128), F32),
                pltpu.VMEM((tiles, rows, 128), jnp.int32),
                pltpu.VMEM((tiles, rows, 128), jnp.int32),
                pltpu.VMEM((6, 128, 128), BF16),
                pltpu.VMEM((2, 2, deep, 128), F32),
                pltpu.VMEM((ext // 4, 128), F32),
                pltpu.VMEM((2, deep, 128), F32),
                pltpu.VMEM((2, ext // 4, 128), F32),
                *exchange_refs(rows, HALO),
                *exchange_refs(rows // 4, DEEP_LANES),
                pltpu.SemaphoreType.DMA((2, 8)),
                pltpu.SemaphoreType.DMA((2, 8)),
                pltpu.SemaphoreType.DMA((3, tiles)),
                pltpu.SemaphoreType.DMA((2, tiles)),
                *level_refs(tiles + 1, ext),
                *level_refs(3, ext // 2),
                *level_refs(2, deep),
            ],
            compiler_params=pltpu.CompilerParams(collective_id=0, has_side_effects=True),
            name="vcycle",
        )(right_side, depth_level, ocean_mask)

    return jax.shard_map(
        local,
        mesh=mesh,
        in_specs=(P("lat", "lon"),) * 3,
        out_specs=(P("lat", "lon"),) * 2,
        check_vma=False,
    )
```

```python
import functools

import jax
import jax.numpy as jnp
from jax import lax
from jax.experimental import pallas as pl
from jax.experimental.pallas import tpu as pltpu
from jax.sharding import PartitionSpec as P

DEPTH_LEVELS = 50
COARSE_SWEEPS = 9
OMEGA = 0.8
SIGMA = 1e-05
HALO = 16
DEEP = 24
DEEP_LANES = 32
MESH = pl.DeviceIdType.MESH
F32 = jnp.float32
BF16 = jnp.bfloat16


def lanes_of(shape=(8, 128)):
    return lax.broadcasted_iota(jnp.int32, shape, 1)


def east_of(tiles):
    if len(tiles) == 1:
        return [pltpu.roll(tiles[0], 127, 1)]
    lane = lanes_of()
    turned = [pltpu.roll(x, 127, 1) for x in tiles]
    return [jnp.where(lane == 127, turned[(t + 1) % len(tiles)], turned[t]) for t in range(len(tiles))]


def west_of(tiles):
    if len(tiles) == 1:
        return [pltpu.roll(tiles[0], 1, 1)]
    lane = lanes_of()
    turned = [pltpu.roll(x, 1, 1) for x in tiles]
    return [jnp.where(lane == 0, turned[t - 1], turned[t]) for t in range(len(tiles))]


def upper(x):
    return pltpu.roll(x, 7, 0)


def lower(x):
    return pltpu.roll(x, 1, 0)


def at(j):
    start = (j + 1) * 8
    return pl.ds(start if isinstance(start, int) else pl.multiple_of(start, 8), 8)


def load(ref, j):
    return [ref[t, at(j), :] for t in range(ref.shape[0])]


def store(ref, j, tiles):
    for t, x in enumerate(tiles):
        ref[t, at(j), :] = x


def each(count, unroll, body):
    if unroll >= count:
        for j in range(count):
            body(j)
    else:
        lax.fori_loop(0, count, lambda j, c: (body(j), c)[1], 0, unroll=unroll)


def wrap(ref, count):
    store(ref, -1, [lower(x) for x in load(ref, count - 1)])
    store(ref, count, [upper(x) for x in load(ref, 0)])


def split_dot(x, mat, parts):
    total = None
    for part in range(parts):
        piece = x.astype(BF16)
        term = jnp.dot(piece, mat, preferred_element_type=F32)
        total = term if total is None else total + term
        if part < parts - 1:
            x = x - piece.astype(F32)
    return total


def shrink(tiles, mats, parts):
    outs = []
    for p in range(len(tiles) // 2):
        outs.append(split_dot(tiles[2 * p], mats[0], parts) + split_dot(tiles[2 * p + 1], mats[1], parts))
    if len(tiles) % 2:
        outs.append(split_dot(tiles[-1], mats[2], parts))
    return outs


def spread(tiles, mats, fine_count, parts):
    outs = []
    for p in range(fine_count // 2):
        outs += [split_dot(tiles[p], mats[3], parts), split_dot(tiles[p], mats[4], parts)]
    if fine_count % 2:
        outs.append(split_dot(tiles[fine_count // 2], mats[5], parts))
    return outs


class Level:
    def __init__(self, index, count, unroll, refs):
        self.scale = 0.0625**index / DEPTH_LEVELS
        self.count, self.unroll = count, unroll
        self.h, self.s, self.ke, self.kn, self.w, self.d, self.a, self.b, self.half = refs

    def coefficients(self, source_of=None):
        wrap(self.h, self.count)

        def body(j):
            h = load(self.h, j)
            ke = [jnp.minimum(x, y) * self.scale for x, y in zip(h, east_of(h))]
            kw = west_of(ke)
            kn = [jnp.minimum(x, y) * self.scale for x, y in zip(h, load(self.h, j + 1))]
            ks = [jnp.minimum(x, y) * self.scale for x, y in zip(h, load(self.h, j - 1))]
            faces = [a + b + c + d for a, b, c, d in zip(ke, kw, kn, ks)]
            diag = [SIGMA + f for f in faces]
            w = [OMEGA / d for d in diag]
            for ref, value in ((self.ke, ke), (self.kn, kn), (self.w, w), (self.d, diag)):
                store(ref, j, value)
            if source_of is not None:
                s = [jnp.where(f > 0.0, x, 0.0) for f, x in zip(faces, source_of(j))]
                store(self.s, j, s)
                store(self.a, j, [x * y for x, y in zip(w, s)])

        each(self.count, self.unroll, body)
        wrap(self.kn, self.count)

    def pulled(self, ref, j):
        v, ke = load(ref, j), load(self.ke, j)
        flow = west_of([x * y for x, y in zip(ke, v)])
        rows = zip(ke, east_of(v), flow, load(self.kn, j), load(ref, j + 1), load(self.kn, j - 1), load(ref, j - 1))
        return v, [k * e + f + n * vn + s * vs for k, e, f, n, vn, s, vs in rows]

    def sweep(self, src, dst):
        wrap(src, self.count)

        def body(j):
            v, acc = self.pulled(src, j)
            new = [(1.0 - OMEGA) * x + w * (s + a) for x, w, s, a in zip(v, load(self.w, j), load(self.s, j), acc)]
            store(dst, j, new)

        each(self.count, self.unroll, body)

    def residual(self, ref, j):
        v, acc = self.pulled(ref, j)
        return [s - d * x + a for s, d, x, a in zip(load(self.s, j), load(self.d, j), v, acc)]

    def halve(self, rows_of, factor):
        def body(j):
            for t, (x, y) in enumerate(zip(rows_of(2 * j), rows_of(2 * j + 1))):
                start = j * 8 if isinstance(j, int) else pl.multiple_of(j * 8, 8)
                self.half[t, pl.ds(start, 8), :] = (x + y) * factor

        each(self.count // 2, self.unroll // 2, body)

    def begin(self, source_of):
        def body(j):
            w, d = load(self.w, j), load(self.d, j)
            s = [jnp.where(x > SIGMA, y, 0.0) for x, y in zip(d, source_of(j))]
            store(self.s, j, s)
            store(self.a, j, [x * y for x, y in zip(w, s)])

        each(self.count, self.unroll, body)

    def down(self):
        self.sweep(self.a, self.b)
        wrap(self.b, self.count)
        self.halve(lambda j: self.residual(self.b, j), 0.25)

    def up(self):
        def body(j):
            start = j * 8 if isinstance(j, int) else pl.multiple_of(j * 8, 8)
            extra = [self.half[t, pl.ds(start, 8), :] for t in range(self.half.shape[0])]
            for i in (2 * j, 2 * j + 1):
                store(self.b, i, [x + y for x, y in zip(load(self.b, i), extra)])

        each(self.count // 2, self.unroll // 2, body)
        self.sweep(self.b, self.a)
        self.sweep(self.a, self.b)


class Exchange:
    def __init__(self, x, halo, width, refs, sems, fields):
        self.x, self.halo, self.width = x, halo, width
        self.pack, self.got, self.corner = refs
        self.sems, self.fields = sems, fields
        self.part = pl.ds(fields[0], len(fields))
        self.tiles = x.shape[1] - 1
        self.n = x.shape[2] - 2 * halo
        self.groups = 128 // width

    def fill(self):
        lane = lanes_of()
        blocks = range(self.n // 8 // self.groups)
        for side in range(2):
            for f, m in ((f, m) for f in self.fields for m in blocks):
                total = None
                for g in range(self.groups):
                    row = self.halo + 8 * (m * self.groups + g)
                    chunk = self.x[f, 0 if side == 0 else self.tiles - 1, row : row + 8, :]
                    shift = (self.width * g + side * self.width) % 128
                    chunk = pltpu.roll(chunk, shift, 1) if shift else chunk
                    total = chunk if total is None else jnp.where(lane >= self.width * g, chunk, total)
                self.pack[side, f, 8 * m : 8 * m + 8, :] = total

    def start(self, place):
        lat, lon, nlat, nlon = place
        copies = []

        def send(src, dst, dlat, dlon):
            k = len(copies)
            copy = pltpu.make_async_remote_copy(
                src_ref=src,
                dst_ref=dst,
                send_sem=self.sems.at[0, k],
                recv_sem=self.sems.at[1, k],
                device_id={"lat": lax.rem(lat + dlat + nlat, nlat), "lon": lax.rem(lon + dlon + nlon, nlon)},
                device_id_type=MESH,
            )
            copy.start()
            copies.append(copy)

        h, n, last, p = self.halo, self.n, self.pack.shape[2] - 8, self.part
        for side, dlon in ((0, -1), (1, 1)):
            send(self.pack.at[side, p], self.got.at[side, p], 0, dlon)
        for side, dlon in ((0, -1), (1, 1)):
            send(self.pack.at[side, p, pl.ds(last, 8), :], self.corner.at[side, p], 1, dlon)
            send(self.pack.at[side, p, pl.ds(0, 8), :], self.corner.at[2 + side, p], -1, dlon)
        core = pl.ds(0, self.tiles)
        send(self.x.at[p, core, pl.ds(n, h), :], self.x.at[p, core, pl.ds(0, h), :], 1, 0)
        send(self.x.at[p, core, pl.ds(h, h), :], self.x.at[p, core, pl.ds(h + n, h), :], -1, 0)
        self.copies = copies

    def finish(self, place):
        lat, lon, nlat, nlon = place
        for copy in self.copies:
            copy.wait()
        lane = lanes_of()
        edge, total = self.halo // 8, self.x.shape[2] // 8
        count = self.n // 8
        for f in self.fields:
            for b in range(total):
                a = b - edge
                if a < 0:
                    a, refs = a + count, (self.corner.at[0, f], self.corner.at[1, f])
                    start = 0
                elif a >= count:
                    a, refs = a - count, (self.corner.at[2, f], self.corner.at[3, f])
                    start = 0
                else:
                    start = 8 * (a // self.groups)
                    refs = (self.got.at[0, f], self.got.at[1, f])
                g = a % self.groups
                east, west = refs[0][start : start + 8, :], refs[1][start : start + 8, :]
                shift = (128 - self.width * g) % 128
                east = pltpu.roll(east, shift, 1) if shift else east
                shift = (256 - self.width - self.width * g) % 128
                west = pltpu.roll(west, shift, 1) if shift else west
                tile = jnp.where(lane < self.width, east, jnp.where(lane >= 128 - self.width, west, 0.0))
                self.x[f, self.tiles, 8 * b : 8 * b + 8, :] = tile
        for blocks, pole in ((range(edge), lat == 0), (range(total - edge, total), lat == nlat - 1)):
            keep = jnp.where(pole, 0.0, 1.0)
            for f in self.fields:
                for t in range(self.tiles + 1):
                    for b in blocks:
                        self.x[f, t, 8 * b : 8 * b + 8, :] = self.x[f, t, 8 * b : 8 * b + 8, :] * keep


def kernel(place_of, right_hbm, depth_hbm, mask_hbm, out, x0, depth, mask, mats, x2, y2, z2, c1, hp, hq, *rest):
    nlat, nlon = place_of
    pack0, got0, corner0, pack2, got2, corner2, sems0, sems2, in_sems, sems1 = rest[:10]
    refs0, refs1, refs2 = rest[10:19], rest[19:28], rest[28:37]
    lat, lon = lax.axis_index("lat"), lax.axis_index("lon")
    place = (lat, lon, nlat, nlon)
    rows = depth.shape[1]
    tiles = depth.shape[0]

    loads = []
    for t in range(tiles):
        cols = pl.ds(128 * t, 128)
        for i, (src, dst) in enumerate(
            (
                (depth_hbm.at[:, cols], depth.at[t]),
                (mask_hbm.at[:, cols], mask.at[t]),
                (right_hbm.at[:, cols], x0.at[1, t, pl.ds(HALO, rows), :]),
            )
        ):
            loads.append(pltpu.make_async_copy(src, dst, in_sems.at[i, t]))
            loads[-1].start()

    barrier = pltpu.get_barrier_semaphore()
    for dlat in (-1, 0, 1):
        for dlon in (-1, 0, 1):
            if dlat or dlon:
                pl.semaphore_signal(
                    barrier,
                    inc=1,
                    device_id={"lat": lax.rem(lat + dlat + nlat, nlat), "lon": lax.rem(lon + dlon + nlon, nlon)},
                    device_id_type=MESH,
                )

    fine = lax.broadcasted_iota(jnp.int32, (128, 128), 0)
    coarse = lanes_of((128, 128))
    for base, f, c in ((0, fine, coarse), (3, coarse, fine)):
        first = jnp.right_shift(f, 1)
        for i, target in enumerate((first, first + 64, jnp.where(f < 64, first, first + 64))):
            mats[base + i] = jnp.where(target == c, 1.0, 0.0).astype(BF16)
    mats = [mats[i] for i in range(6)]

    for copy in loads:
        copy.wait()
    for t in range(tiles):
        x0[0, t, HALO : HALO + rows, :] = (depth[t] * mask[t]).astype(F32)
    outer = Exchange(x0, HALO, HALO, (pack0, got0, corner0), sems0, (0, 1))
    outer.fill()
    pl.semaphore_wait(barrier, 8)
    outer.start(place)

    for t in range(tiles):
        for a in range(rows // 16):
            pair = [x0[0, t, pl.ds(HALO + 16 * a + i, 8, stride=2), :] for i in range(2)]
            hp[t, 8 * a : 8 * a + 8, :] = pair[0] + pair[1]
    for t, x in enumerate(shrink([hp[t] for t in range(tiles)], mats, 1)):
        hq[t] = x
    for t in range(tiles // 2):
        for a in range(rows // 32):
            pair = [hq[t, pl.ds(16 * a + i, 8, stride=2), :] for i in range(2)]
            hp[t, 8 * a : 8 * a + 8, :] = pair[0] + pair[1]
    deep_rows = rows // 4
    x2[0, 0, DEEP : DEEP + deep_rows, :] = shrink([hp[t, 0:deep_rows, :] for t in range(2)], mats, 2)[0]
    deep_height = Exchange(x2, DEEP, DEEP_LANES, (pack2, got2, corner2), sems1, (0,))
    deep_height.fill()
    deep_height.start(place)
    outer.finish(place)

    count0 = refs0[0].shape[1] // 8 - 2
    count1 = refs1[0].shape[1] // 8 - 2
    count2 = refs2[0].shape[1] // 8 - 2
    level0 = Level(0, count0, 12, refs0)
    level1 = Level(1, count1, 18, refs1)
    level2 = Level(2, count2, count2, refs2)
    for j in range(count0):
        for t in range(tiles + 1):
            level0.h[t, at(j), :] = x0[0, t, pl.ds(j, 8, stride=count0), :]

    level0.halve(lambda j: load(level0.h, j), 1.0)
    for t, x in enumerate(shrink([level0.half[t] for t in range(tiles + 1)], mats, 1)):
        level1.h[t, 8 : 8 + 8 * count1, :] = x
    level0.coefficients(lambda j: [x0[1, t, pl.ds(j, 8, stride=count0), :] for t in range(tiles + 1)])
    level0.down()
    for t, x in enumerate(shrink([level0.half[t] for t in range(tiles + 1)], mats, 3)):
        level1.s[t, 8 : 8 + 8 * count1, :] = x

    half1 = count1 // 2
    margin = HALO // 4
    level1.coefficients(lambda j: load(level1.s, j))
    level1.down()
    fallen = shrink([level1.half[0], level1.half[1]], mats, 3)[0]
    for j in range(half1):
        y2[pl.ds(j, 8, stride=half1), :] = fallen[8 * j : 8 * j + 8]
    for a in range(deep_rows // 8):
        x2[1, 0, DEEP + 8 * a : DEEP + 8 * a + 8, :] = y2[margin + 8 * a : margin + 8 * a + 8, :]

    inner = Exchange(x2, DEEP, DEEP_LANES, (pack2, got2, corner2), sems2, (1,))
    inner.fill()
    inner.start(place)
    deep_height.finish(place)
    for j in range(count2):
        for t in range(2):
            level2.h[t, at(j), :] = x2[0, t, pl.ds(j, 8, stride=count2), :]
    count3 = count2 // 2
    level2.coefficients()
    level2.halve(lambda j: load(level2.h, j), 1.0)
    height = shrink([level2.half[0], level2.half[1]], mats, 2)[0]

    scale = 0.0625**3 / DEPTH_LEVELS
    h = [height[8 * j : 8 * j + 8] for j in range(count3)]

    def north(v):
        return v[1:] + [upper(v[0])]

    ke = [jnp.minimum(x, pltpu.roll(x, 127, 1)) * scale for x in h]
    kn = [jnp.minimum(x, y) * scale for x, y in zip(h, north(h))]
    ks = [lower(kn[-1])] + kn[:-1]
    faces = [a + pltpu.roll(a, 1, 1) + b + c for a, b, c in zip(ke, kn, ks)]
    w = [OMEGA / (SIGMA + f) for f in faces]

    inner.finish(place)
    level2.begin(lambda j: [x2[1, t, pl.ds(j, 8, stride=count2), :] for t in range(2)])
    level2.down()
    source = shrink([level2.half[0], level2.half[1]], mats, 3)[0]
    s = [jnp.where(f > 0.0, source[8 * j : 8 * j + 8], 0.0) for j, f in enumerate(faces)]
    v = [x * y for x, y in zip(w, s)]
    for _ in range(COARSE_SWEEPS - 1):
        up, down = north(v), [lower(v[-1])] + v[:-1]
        v = [
            (1.0 - OMEGA) * v[j]
            + w[j]
            * (s[j] + ke[j] * pltpu.roll(v[j], 127, 1) + pltpu.roll(ke[j] * v[j], 1, 1) + kn[j] * up[j] + ks[j] * down[j])
            for j in range(count3)
        ]

    for t, x in enumerate(spread([jnp.concatenate(v, axis=0)], mats, 2, 3)):
        level2.half[t] = x
    level2.up()
    for j in range(count2):
        for t in range(2):
            z2[t, pl.ds(j, 8, stride=count2), :] = level2.b[t, at(j), :]
    for j in range(half1):
        for t in range(2):
            c1[t, 8 * j : 8 * j + 8, :] = z2[t, pl.ds(DEEP - margin + j, 8, stride=half1), :]
    for t, x in enumerate(spread([c1[0], c1[1]], mats, 3, 3)):
        level1.half[t] = x
    level1.up()
    body = pl.ds(8, 8 * count1)
    for t, x in enumerate(spread([level1.b[t, body, :] for t in range(3)], mats, tiles + 1, 3)):
        level0.half[t] = x
    level0.up()
    wrap(level0.b, count0)

    def last(j):
        pressure, residual = load(level0.b, j), level0.residual(level0.b, j)
        for t in range(tiles):
            out[0, t, pl.ds(j, 8, stride=count0), :] = pressure[t]
            out[1, t, pl.ds(j, 8, stride=count0), :] = residual[t]

    each(count0, level0.unroll, last)


def hand_out(out, press_hbm, resid_hbm, sems):
    rows = press_hbm.shape[0]
    stores = []
    for i, ref in enumerate((press_hbm, resid_hbm)):
        for t in range(out.shape[1]):
            src = out.at[i, t, pl.ds((out.shape[2] - rows) // 2, rows), :]
            stores.append(pltpu.make_async_copy(src, ref.at[:, pl.ds(128 * t, 128)], sems.at[i, t]))
            stores[-1].start()
    for copy in stores:
        copy.wait()


def solution(mesh):
    nlat, nlon = mesh.shape["lat"], mesh.shape["lon"]

    def local(right_side, depth_level, ocean_mask):
        rows, columns = right_side.shape
        tiles = columns // 128
        ext = rows + 2 * HALO
        deep = rows // 4 + 2 * DEEP

        def level_refs(tiles, total):
            full = pltpu.VMEM((tiles, total + 16, 128), F32)
            return [full] * 8 + [pltpu.VMEM((tiles, total // 2, 128), F32)]

        def exchange_refs(n, width):
            packed = pltpu.VMEM((2, 2, n * width // 128, 128), F32)
            return [packed, packed, pltpu.VMEM((4, 2, 8, 128), F32)]

        both = pl.pallas_call(
            functools.partial(kernel, (nlat, nlon)),
            out_shape=pltpu.VMEM((2, tiles, ext, 128), F32),
            in_specs=[pl.BlockSpec(memory_space=pl.ANY)] * 3,
            out_specs=pl.BlockSpec(memory_space=pltpu.VMEM),
            scratch_shapes=[
                pltpu.VMEM((2, tiles + 1, ext, 128), F32),
                pltpu.VMEM((tiles, rows, 128), jnp.int32),
                pltpu.VMEM((tiles, rows, 128), jnp.int32),
                pltpu.VMEM((6, 128, 128), BF16),
                pltpu.VMEM((2, 2, deep, 128), F32),
                pltpu.VMEM((ext // 4, 128), F32),
                pltpu.VMEM((2, deep, 128), F32),
                pltpu.VMEM((2, ext // 4, 128), F32),
                pltpu.VMEM((tiles, rows // 2, 128), F32),
                pltpu.VMEM((tiles // 2, rows // 2, 128), F32),
                *exchange_refs(rows, HALO),
                *exchange_refs(rows // 4, DEEP_LANES),
                pltpu.SemaphoreType.DMA((2, 8)),
                pltpu.SemaphoreType.DMA((2, 8)),
                pltpu.SemaphoreType.DMA((3, tiles)),
                pltpu.SemaphoreType.DMA((2, 8)),
                *level_refs(tiles + 1, ext),
                *level_refs(3, ext // 2),
                *level_refs(2, deep),
            ],
            compiler_params=pltpu.CompilerParams(collective_id=0, has_side_effects=True, vmem_limit_bytes=67_043_328 - (2 * tiles * ext + 256) * 512),
            name="vcycle",
        )(right_side, depth_level, ocean_mask)
        return pl.pallas_call(
            hand_out,
            out_shape=[jax.ShapeDtypeStruct((rows, columns), F32)] * 2,
            in_specs=[pl.BlockSpec(memory_space=pltpu.VMEM)],
            out_specs=[pl.BlockSpec(memory_space=pl.ANY)] * 2,
            scratch_shapes=[pltpu.SemaphoreType.DMA((2, tiles))],
            compiler_params=pltpu.CompilerParams(vmem_limit_bytes=8 * 2**20),
            name="hand_out",
        )(both)

    return jax.shard_map(
        local,
        mesh=mesh,
        in_specs=(P("lat", "lon"),) * 3,
        out_specs=(P("lat", "lon"),) * 2,
        check_vma=False,
    )
```
